32 devices in a mesh: gx: 8 (over z, y), gy: 2 (over x), col: 2 (over core).
Axes of the slice: x: 2, y: 2, z: 4, core: 2. Of those that a mesh axis runs over, the one named last changes fastest.
Arguments:
- particles: float32 [22, 8, 32, 12, 256], P(None, None, 'gx', 'gy', 'col'), may hold values from -1.6 to 1.6, as said below
- masses: float32 [8, 32, 12, 256], P(None, 'gx', 'gy', 'col'), may hold values from 0.06 to 0.19
- occupied: int32 [8, 32, 12, 256], P(None, 'gx', 'gy', 'col'), may hold values from 0 to 1, as said below
- node_flags: int32 [32, 12, 256], P('gx', 'gy', 'col'), may hold values from 0 to 2, as said below
- depart: int32 [8, 2, 2, 8, 128], P('gx', 'gy', 'col'), may hold values from 0 to 24575, as said below
- arrive: int32 [8, 2, 2, 8, 128], P('gx', 'gy', 'col'), may hold values from 0 to 3071, as said below
Outputs:
- final_state: float32 [9, 8, 32, 12, 256], P(None, None, 'gx', 'gy', 'col')
- arrivals: float32 [9, 8, 2, 2, 1024], P(None, 'gx', 'gy', 'col')
The draws below stay inside these ranges and needn't reach their ends.
Inputs may be any that keep to these rules, and one draw needn't show every extreme that they name: `particles`: offsets lie in -0.5 .. 0.5; a particle listed in depart for direction (dx, dy) has its offset's x component between 0.4 and 0.5 times dx where dx is not 0, and likewise y; volumes lie in 0.08 .. 0.16. The scaffold fills some aligned 4 x 4 x 4 blocks of cells and leaves the others empty; in filled blocks most slots are occupied. `node_flags`: in every (x, y) column the lowest 1 to 3 nodes are 1 and the highest 1 to 3 nodes are 2; all others are 0. `depart`: all 1024 entries of a block are distinct; an entry for direction (dx, dy) names a slot of a cell with i = 3 where dx = 1, i = 0 where dx = -1, j = 5 where dy = 1, j = 0 where dy = -1. Some named slots are empty. arrive[b', d, e] is the cell (i * 6 + j) * 128 + k of block b' that lies across the block boundary from the cell of depart[b' - (dx, dy), d, e], moved by (dx, dy) with the same k.
All inputs are finite; a program needn't handle non-finite values.
Results may differ from the reference program's by a relative error of at most 0.0001.
Values sent between devices are 32-bit elements; how exact they have to be, the bound alone decides.
A program may use at most 128 MiB of HBM per device.

```python
import jax
import jax.numpy as jnp
import numpy as np
from jax import lax

CX = 4
CY = 6
CZ = 128
K = 128
SLOTS = 8
DIRS = 8
STATE = 22
REPORT = 9
NX = 32
NY = 12
NZ = 256
N_GX = 8
N_GY = 2
N_COL = 2


SHIFT_X = (-1, -1, -1, 0, 0, 1, 1, 1)


SHIFT_Y = (-1, 0, 1, -1, 1, -1, 0, 1)


def mover_labels():
    running = SLOTS * CX * CY * CZ
    flattened = np.arange(running)
    slot_index = flattened // (CX * CY * CZ)
    cell_index = flattened % (CX * CY * CZ)
    row_x = cell_index // (CY * CZ)
    row_y = cell_index // CZ % CY
    side_x = np.where(row_x == CX - 1, 1, np.where(row_x == 0, -1, 0))
    side_y = np.where(row_y == CY - 1, 1, np.where(row_y == 0, -1, 0))
    corner = (side_x != 0) & (side_y != 0)
    step_x = np.where(corner & (slot_index >= 6), 0, side_x)
    step_y = np.where(corner & (slot_index >= 4) & (slot_index < 6), 0, side_y)
    direction_code = (step_x + 1) * 3 + step_y + 1
    labels = np.where(direction_code == 4, -1, direction_code - (direction_code > 4))
    landing_x = row_x + step_x - step_x * CX
    landing_y = row_y + step_y - step_y * CY
    landing = (landing_x * CY + landing_y) * CZ + cell_index % CZ
    return (labels, landing)


def mover_lists(key):
    labels, landing = mover_labels()
    running = labels.shape[0]
    devices = NX // CX * (NY // CY) * (NZ // CZ)
    spread_max = max(2, 2 ** 30 // running)
    flattened = jnp.arange(running, dtype=jnp.int32)
    chosen = []
    for d in range(8):
        scores = jax.random.randint(jax.random.fold_in(key, d), (devices, running), 0, spread_max, dtype=jnp.int32) * running + flattened
        scores = jnp.where(jnp.asarray(labels == d)[None], scores, -1 - flattened)
        winners = lax.top_k(scores, K)[1]
        chosen.append(winners.astype(jnp.int32))
    depart = jnp.stack(chosen, axis=1).reshape(NX // CX, NY // CY, NZ // CZ, 8, K)
    landed = jnp.asarray(landing.astype(np.int32))[depart]
    arrive = jnp.stack([jnp.roll(landed[:, :, :, d], (SHIFT_X[d], SHIFT_Y[d]), axis=(0, 1)) for d in range(8)], axis=3)
    return (depart, arrive.astype(jnp.int32))


def draw_depart(key, part):
    return mover_lists(jax.random.fold_in(key, 7))[0]


def draw_arrive(key, part):
    return mover_lists(jax.random.fold_in(key, 7))[1]


def spread_out(marks):
    shaped = marks.reshape(NX // CX, NY // CY, NZ // CZ, SLOTS, CX, CY, CZ)
    return shaped.transpose(3, 0, 4, 1, 5, 2, 6).reshape(SLOTS, NX, NY, NZ)


def draw_particles(key, part):
    depart, unused = mover_lists(jax.random.fold_in(key, 7))
    devices = depart.shape[0] * depart.shape[1] * depart.shape[2]
    running = SLOTS * CX * CY * CZ
    leaving = depart.reshape(devices, 8, K)
    device_rows = jnp.arange(devices)[:, None]
    marks_x = jnp.zeros((devices, running), jnp.float32)
    marks_y = jnp.zeros((devices, running), jnp.float32)
    for d in range(8):
        marks_x = marks_x.at[device_rows, leaving[:, d]].set(float(SHIFT_X[d]))
        marks_y = marks_y.at[device_rows, leaving[:, d]].set(float(SHIFT_Y[d]))
    marks_x = spread_out(marks_x)
    marks_y = spread_out(marks_y)
    grid_shape = (SLOTS, NX, NY, NZ)
    subkeys = jax.random.split(jax.random.fold_in(key, 3), 6)
    offset = jax.random.uniform(subkeys[0], (3,) + grid_shape, jnp.float32, -0.5, 0.5)
    velocity = jnp.clip(0.3 * jax.random.normal(subkeys[1], (3,) + grid_shape, jnp.float32), -1.2, 1.2)
    gradient = jnp.clip(0.3 * jax.random.normal(subkeys[2], (9,) + grid_shape, jnp.float32), -1.2, 1.2)
    stress = jnp.clip(0.5 * jax.random.normal(subkeys[3], (6,) + grid_shape, jnp.float32), -1.6, 1.6)
    volume = jax.random.uniform(subkeys[4], (1,) + grid_shape, jnp.float32, 0.08, 0.16)
    leaning = jax.random.uniform(subkeys[5], (2,) + grid_shape, jnp.float32, 0.4, 0.5)
    along_x = jnp.where(marks_x != 0.0, marks_x * leaning[0], offset[0])
    along_y = jnp.where(marks_y != 0.0, marks_y * leaning[1], offset[1])
    return jnp.concatenate([along_x[None], along_y[None], offset[2:3], velocity, gradient, stress, volume]).astype(jnp.float32)


def draw_occupied(key, part):
    subkeys = jax.random.split(jax.random.fold_in(key, 5), 2)
    blocks = jax.random.randint(subkeys[0], ((NX + 3) // 4, (NY + 3) // 4, (NZ + 3) // 4), 0, 2, dtype=jnp.int32)
    solidity = jnp.take(jnp.take(jnp.take(blocks, jnp.arange(NX) // 4, axis=0), jnp.arange(NY) // 4, axis=1), jnp.arange(NZ) // 4, axis=2)
    filled = jax.random.randint(subkeys[1], (SLOTS, NX, NY, NZ), 0, 8, dtype=jnp.int32) < 7
    return (solidity[None] * filled.astype(jnp.int32)).astype(jnp.int32)


def draw_node_flags(key, part):
    subkeys = jax.random.split(jax.random.fold_in(key, 9), 2)
    bottom = jax.random.randint(subkeys[0], (NX, NY, 1), 1, 4, dtype=jnp.int32)
    top_depth = jax.random.randint(subkeys[1], (NX, NY, 1), 1, 4, dtype=jnp.int32)
    height = jnp.arange(NZ, dtype=jnp.int32)[None, None, :]
    return jnp.where(height < bottom, 1, jnp.where(height >= NZ - top_depth, 2, 0)).astype(jnp.int32)


def steps_of(own_key, extent, cuts, least, high):
    level, own = 1.0, jax.random.fold_in(own_key, 6)
    for position, shards_of in cuts:
        steps = jnp.exp(jax.random.uniform(jax.random.fold_in(own, position), (shards_of,), jnp.float32, least / len(cuts), high / len(cuts)))
        level = level * jnp.repeat(steps, extent[position] // shards_of).reshape([-1 if axis == position else 1 for axis in range(len(extent))])
    return level


def setup_inputs(seed: int = 0) -> dict:
    key_list = jax.random.split(jax.random.key(seed), 7)
    particles = draw_particles(jax.random.fold_in(key_list[6], 71), 0)
    masses = jnp.clip(0.06 + 0.13 * jax.random.uniform(key_list[1], (SLOTS, NX, NY, NZ), jnp.float32) ** steps_of(key_list[1], (SLOTS, NX, NY, NZ), ((1, 8), (2, 2), (3, 2)), -0.2, 0.2), 0.06, 0.19)
    occupied = draw_occupied(jax.random.fold_in(key_list[6], 71), 0)
    node_flags = draw_node_flags(jax.random.fold_in(key_list[6], 71), 0)
    depart = draw_depart(jax.random.fold_in(key_list[6], 71), 0)
    arrive = draw_arrive(jax.random.fold_in(key_list[6], 71), 0)
    return dict(particles=particles, masses=masses, occupied=occupied, node_flags=node_flags, depart=depart, arrive=arrive)


TIME_STEP = 0.2
LAME_FIRST = 2.5
SHEAR_MODULUS = 2.5
YIELD_STRESS = 1.2
MASS_FLOOR = 0.1
PLATEN_SPEED = 0.5
SHIFT_X = (-1, -1, -1, 0, 0, 1, 1, 1)
SHIFT_Y = (-1, 0, 1, -1, 1, -1, 0, 1)
STRESS_SLOT = ((0, 5, 4), (5, 1, 3), (4, 3, 2))
STRESS_PAIRS = ((0, 0), (1, 1), (2, 2), (1, 2), (0, 2), (0, 1))

def spline_weights(offset):
    left_weight = 0.5 * (0.5 - offset) * (0.5 - offset)
    centre_weight = 0.75 - offset * offset
    right_weight = 0.5 * (0.5 + offset) * (0.5 + offset)
    return jnp.stack([left_weight, centre_weight, right_weight], axis=1)

def particle_terms(record, mass_eff, vol_eff):
    offset = record[0:3]
    affine = [[mass_eff * record[6 + 3 * k + b] - 4.0 * TIME_STEP * vol_eff * record[15 + STRESS_SLOT[k][b]] for b in range(3)] for k in range(3)]
    anchor = [mass_eff * record[3 + k] - (affine[k][0] * offset[0] + affine[k][1] * offset[1] + affine[k][2] * offset[2]) for k in range(3)]
    return jnp.stack([mass_eff] + anchor + [affine[k][b] for k in range(3) for b in range(3)])

def node_momentum(values, offsets):
    return [values[1 + k] + offsets[0] * values[4 + 3 * k] + offsets[1] * values[5 + 3 * k] + offsets[2] * values[6 + 3 * k] for k in range(3)]

def advance(record, new_speed, moments):
    offset = record[0:3]
    gradient = [[4.0 * (moments[b][k] - offset[b] * new_speed[k]) for b in range(3)] for k in range(3)]
    divergence = gradient[0][0] + gradient[1][1] + gradient[2][2]
    trial_stress = []
    for n in range(6):
        k, b = STRESS_PAIRS[n]
        strain = 0.5 * (gradient[k][b] + gradient[b][k])
        change = 2.0 * SHEAR_MODULUS * strain
        if k == b:
            change = change + LAME_FIRST * divergence
        trial_stress.append(record[15 + n] + TIME_STEP * change)
    pressure = (trial_stress[0] + trial_stress[1] + trial_stress[2]) / 3.0
    deviator = [trial_stress[n] - pressure for n in range(3)] + trial_stress[3:]
    square = deviator[0] * deviator[0] + deviator[1] * deviator[1] + deviator[2] * deviator[2] + 2.0 * (deviator[3] * deviator[3] + deviator[4] * deviator[4] + deviator[5] * deviator[5])
    factor = YIELD_STRESS / jnp.maximum(jnp.sqrt(1.5 * square), YIELD_STRESS)
    stress = [pressure + factor * deviator[n] for n in range(3)] + [factor * deviator[n] for n in range(3, 6)]
    volume = record[21] * (1.0 + TIME_STEP * divergence)
    return jnp.concatenate([offset + TIME_STEP * new_speed, new_speed, jnp.stack([gradient[k][b] for k in range(3) for b in range(3)]), jnp.stack(stress), volume[None]])

def node_velocity(lattice, node_flags):
    velocity = lattice[1:4] / jnp.maximum(lattice[0], MASS_FLOOR)
    velocity = jnp.where(node_flags == 1, 0.0, velocity)
    rising = jnp.where(node_flags == 2, -PLATEN_SPEED, velocity[2])
    return jnp.stack([velocity[0], velocity[1], rising])

def to_blocks(values):
    channels = values.shape[0]
    shaped = values.reshape(channels, SLOTS, N_GX, CX, N_GY, CY, N_COL, CZ)
    return shaped.transpose(2, 4, 6, 0, 1, 3, 5, 7).reshape(N_GX, N_GY, N_COL, channels, SLOTS * CX * CY * CZ)

def from_blocks(blocks):
    channels = blocks.shape[3]
    shaped = blocks.reshape(N_GX, N_GY, N_COL, channels, SLOTS, CX, CY, CZ)
    return shaped.transpose(3, 4, 0, 5, 1, 6, 2, 7).reshape(channels, SLOTS, NX, NY, NZ)

def deposit_slots(record, mass_eff, vol_eff):
    weights = spline_weights(record[0:3])
    values = particle_terms(record, mass_eff, vol_eff)
    lattice = jnp.zeros((4, NX, NY, NZ), jnp.float32)
    for a in range(3):
        for b in range(3):
            for c in range(3):
                spline = weights[0, a] * weights[1, b] * weights[2, c]
                moment = node_momentum(values, (a - 1.0, b - 1.0, c - 1.0))
                summed = jnp.stack([lax.optimization_barrier(jnp.sum(spline * values[0], axis=0))] + [lax.optimization_barrier(jnp.sum(spline * moment[k], axis=0)) for k in range(3)])
                summed = jnp.roll(summed, (a - 1, b - 1), axis=(1, 2))
                lattice = lattice + jnp.pad(summed, ((0, 0), (0, 0), (0, 0), (c, 2 - c)))[:, :, :, 1:NZ + 1]
    return (lattice, weights)

def gather_slots(record, weights, velocity):
    padded = jnp.pad(velocity, ((0, 0), (0, 0), (0, 0), (1, 1)))
    new_speed = jnp.zeros((3,) + record.shape[1:], jnp.float32)
    moments = [new_speed, new_speed, new_speed]
    for a in range(3):
        for b in range(3):
            for c in range(3):
                spline = weights[0, a] * weights[1, b] * weights[2, c]
                nearby = jnp.roll(padded, (1 - a, 1 - b), axis=(1, 2))[:, :, :, c:c + NZ]
                contrib = spline[None] * nearby[:, None]
                new_speed = new_speed + contrib
                moments = [moments[0] + (a - 1.0) * contrib, moments[1] + (b - 1.0) * contrib, moments[2] + (c - 1.0) * contrib]
    return advance(record, new_speed, moments)

def deposit_list(lattice, movers, places):
    weights = spline_weights(movers[0:3])
    values = particle_terms(movers[0:22], movers[22], movers[21] * movers[23])
    flattened = lattice.reshape(4, -1)
    for a in range(3):
        for b in range(3):
            for c in range(3):
                spline = weights[0, a] * weights[1, b] * weights[2, c]
                moment = node_momentum(values, (a - 1.0, b - 1.0, c - 1.0))
                contrib = spline[None] * jnp.stack([values[0]] + moment)
                node_x = (places[0] + (a - 1)) % NX
                node_y = (places[1] + (b - 1)) % NY
                node_z = places[2] + (c - 1)
                inside = ((node_z >= 0) & (node_z < NZ)).astype(jnp.float32)
                node_index = ((node_x * NY + node_y) * NZ + jnp.clip(node_z, 0, NZ - 1)).astype(jnp.int32)
                flattened = flattened.at[:, node_index].add(contrib * inside)
    return (flattened.reshape(lattice.shape), weights)

def gather_list(record, weights, velocity, places):
    flattened = jnp.pad(velocity, ((0, 0), (0, 0), (0, 0), (1, 1))).reshape(3, -1)
    new_speed = jnp.zeros((3, record.shape[1]), jnp.float32)
    moments = [new_speed, new_speed, new_speed]
    for a in range(3):
        for b in range(3):
            for c in range(3):
                spline = weights[0, a] * weights[1, b] * weights[2, c]
                node_x = (places[0] + (a - 1)) % NX
                node_y = (places[1] + (b - 1)) % NY
                node_index = ((node_x * NY + node_y) * (NZ + 2) + places[2] + c).astype(jnp.int32)
                nearby = jnp.take(flattened, node_index, axis=1)
                contrib = spline[None] * nearby
                new_speed = new_speed + contrib
                moments = [moments[0] + (a - 1.0) * contrib, moments[1] + (b - 1.0) * contrib, moments[2] + (c - 1.0) * contrib]
    return advance(record, new_speed, moments)

def reference(particles, masses, occupied, node_flags, depart, arrive):
    occupy = occupied.astype(jnp.float32)
    mass_eff = masses * occupy
    lattice, weights = deposit_slots(particles, mass_eff, particles[21] * occupy)
    after_first = gather_slots(particles, weights, node_velocity(lattice, node_flags))
    packed = to_blocks(jnp.concatenate([after_first, mass_eff[None], occupy[None]]))
    moving_count = DIRS * K
    chosen = jnp.broadcast_to(depart.reshape(N_GX, N_GY, N_COL, 1, moving_count), (N_GX, N_GY, N_COL, STATE + 2, moving_count))
    picked = jnp.take_along_axis(packed, chosen, axis=4).reshape(N_GX, N_GY, N_COL, STATE + 2, DIRS, K)
    step_x = jnp.array(SHIFT_X, jnp.float32)[:, None]
    step_y = jnp.array(SHIFT_Y, jnp.float32)[:, None]
    picked = jnp.concatenate([picked[:, :, :, 0:1] - step_x, picked[:, :, :, 1:2] - step_y, picked[:, :, :, 2:]], axis=3)
    arrived = jnp.stack([jnp.roll(picked[:, :, :, :, d], (SHIFT_X[d], SHIFT_Y[d]), axis=(0, 1)) for d in range(DIRS)], axis=4)
    movers = arrived.transpose(3, 0, 1, 2, 4, 5).reshape(STATE + 2, -1)
    blocked = to_blocks(occupy[None])[:, :, :, 0]
    remain_blocks = jax.vmap(lambda occupancy_row, departed: occupancy_row.at[departed].set(0.0))(blocked.reshape(-1, blocked.shape[-1]), depart.reshape(-1, moving_count))
    remain = from_blocks(remain_blocks.reshape(N_GX, N_GY, N_COL, 1, -1))[0]
    cell_x = arrive // (CY * CZ) + (jnp.arange(N_GX, dtype=jnp.int32) * CX)[:, None, None, None, None]
    cell_y = arrive // CZ % CY + (jnp.arange(N_GY, dtype=jnp.int32) * CY)[None, :, None, None, None]
    cell_z = arrive % CZ + (jnp.arange(N_COL, dtype=jnp.int32) * CZ)[None, None, :, None, None]
    places = (cell_x.reshape(-1).astype(jnp.int32), cell_y.reshape(-1).astype(jnp.int32), cell_z.reshape(-1).astype(jnp.int32))
    lattice, weights = deposit_slots(after_first, masses * remain, after_first[21] * remain)
    lattice, mover_weights = deposit_list(lattice, movers, places)
    velocity = node_velocity(lattice, node_flags)
    second = gather_slots(after_first, weights, velocity)
    moved_on = gather_list(movers[0:STATE], mover_weights, velocity, places)
    final_state = jnp.concatenate([second[3:6], second[15:21]]) * remain
    report = (jnp.concatenate([moved_on[3:6], moved_on[15:21]]) * movers[STATE + 1]).reshape(REPORT, N_GX, N_GY, N_COL, moving_count)
    return (final_state, report)
```

```python
import functools

import jax
import jax.numpy as jnp
from jax import lax
from jax.experimental import pallas as pl
from jax.experimental.pallas import tpu as pltpu
from jax.sharding import PartitionSpec as P

TIME_STEP = 0.2
LAME_FIRST = 2.5
SHEAR_MODULUS = 2.5
YIELD_STRESS = 1.2
MASS_FLOOR = 0.1
PLATEN_SPEED = 0.5
SHIFT_X = (-1, -1, -1, 0, 0, 1, 1, 1)
SHIFT_Y = (-1, 0, 1, -1, 1, -1, 0, 1)
STRESS_SLOT = ((0, 5, 4), (5, 1, 3), (4, 3, 2))
STRESS_PAIRS = ((0, 0), (1, 1), (2, 2), (1, 2), (0, 2), (0, 1))
F32 = jnp.float32


def spline(u):
    lo = 0.5 - u
    hi = 0.5 + u
    return (0.5 * lo * lo, 0.75 - u * u, 0.5 * hi * hi)


def advance(state, speed, moments):
    offset = state[0:3]
    grad = [[4.0 * (moments[b][k] - offset[b] * speed[k]) for b in range(3)] for k in range(3)]
    div = grad[0][0] + grad[1][1] + grad[2][2]
    trial = []
    for n in range(6):
        k, b = STRESS_PAIRS[n]
        if k == b:
            change = 2.0 * SHEAR_MODULUS * grad[k][k] + LAME_FIRST * div
        else:
            change = SHEAR_MODULUS * (grad[k][b] + grad[b][k])
        trial.append(state[15 + n] + TIME_STEP * change)
    pressure = (trial[0] + trial[1] + trial[2]) / 3.0
    dev = [trial[n] - pressure for n in range(3)] + trial[3:]
    square = (
        dev[0] * dev[0]
        + dev[1] * dev[1]
        + dev[2] * dev[2]
        + 2.0 * (dev[3] * dev[3] + dev[4] * dev[4] + dev[5] * dev[5])
    )
    factor = YIELD_STRESS / jnp.maximum(jnp.sqrt(1.5 * square), YIELD_STRESS)
    stress = [pressure + factor * dev[n] for n in range(3)] + [factor * dev[n] for n in range(3, 6)]
    return grad, div, stress


def kernel(
    S, X, Y, n_gx, n_gy,
    part, mass, occ, flags, rowq, kidx,
    out, arr,
    ST, PT, D, GZ, N0, N1, FL, VZ, VS, VALS, DM,
    PK, PKR, SYH0, SYL0, RYL0, RYH0, SYH1, SYL1, RYL1, RYH1,
    RXL0, RXH0, RXL1, RXH1, RES, ARR,
    send_sem, recv_sem,
):
    XE, YE = X + 4, Y + 4
    Z = 128
    R = S * X
    gx = lax.axis_index("gx")
    gy = lax.axis_index("gy")
    col = lax.axis_index("col")

    def at(dx, dy):
        return (lax.rem(gx + dx + n_gx, n_gx), lax.rem(gy + dy + n_gy, n_gy), col)

    sibling = (gx, gy, 1 - col)

    barrier = pltpu.get_barrier_semaphore()
    for dx, dy in zip(SHIFT_X, SHIFT_Y):
        pl.semaphore_signal(
            barrier, inc=1, device_id=at(dx, dy), device_id_type=pl.DeviceIdType.MESH
        )
    pl.semaphore_signal(barrier, inc=1, device_id=sibling, device_id_type=pl.DeviceIdType.MESH)

    def send(src, dst, slot, target):
        copy = pltpu.make_async_remote_copy(
            src_ref=src,
            dst_ref=dst,
            send_sem=send_sem.at[slot],
            recv_sem=recv_sem.at[slot],
            device_id=target,
            device_id_type=pl.DeviceIdType.MESH,
        )
        copy.start()
        return copy

    lane = lax.broadcasted_iota(jnp.int32, (YE, Z), 1)
    is_low = (lane * 0 + col) == 0
    row = lax.broadcasted_iota(jnp.int32, (Y, Z), 0)
    far_y = jnp.where(row == 0, -2.0, 2.0).astype(F32)

    def prepare(step):
        def body(q, carry):
            i = q // S
            s = q % S
            r = s * X + i
            if step == 0:
                st = [part[c, r] for c in range(22)]
            else:
                st = [ST[c, q] for c in range(22)]
            o = occ[r].astype(F32)
            m = mass[r] * o
            w = (4.0 * TIME_STEP) * (st[21] * o)
            ws = [w * st[15 + n] for n in range(6)]
            Q = [[m * st[6 + 3 * k + b] - ws[STRESS_SLOT[k][b]] for b in range(3)] for k in range(3)]
            anchor = [
                m * st[3 + k] - (Q[k][0] * st[0] + Q[k][1] * st[1] + Q[k][2] * st[2])
                for k in range(3)
            ]
            PT[0, q] = m
            for k in range(3):
                PT[1 + k, q] = anchor[k]
                for b in range(3):
                    PT[4 + 3 * k + b, q] = Q[k][b]
            if step == 0:
                for dim, base in ((0, 13), (1, 17)):
                    ws3 = spline(st[dim])
                    for e in range(3):
                        PT[base + e, q] = ws3[e]
            else:
                code = DM[q, 0:Y]
                zero = jnp.zeros_like(code)
                sx = jnp.where(code < 3.5, -1.0, jnp.where(code > 5.5, 1.0, 0.0))
                sx = jnp.where(code < 0.5, 0.0, sx)
                low_y = (code == 1.0) | (code == 4.0) | (code == 6.0)
                high_y = (code == 3.0) | (code == 5.0) | (code == 8.0)
                sy = jnp.where(low_y, -1.0, jnp.where(high_y, 1.0, 0.0))
                for dim, base, sh in ((0, 13, sx), (1, 17, sy)):
                    p0, p1, p2 = spline(st[dim] - sh)
                    up = sh > 0.5
                    down = sh < -0.5
                    PT[base, q] = jnp.where(up, zero, jnp.where(down, p1, p0))
                    PT[base + 1, q] = jnp.where(up, p0, jnp.where(down, p2, p1))
                    PT[base + 2, q] = jnp.where(up, p1, jnp.where(down, zero, p2))
                    PT[base + 3, q] = jnp.where(up, p2, jnp.where(down, p0, zero))
            wz = spline(st[2])
            for e in range(3):
                PT[21 + e, q] = wz[e]
            return carry

        lax.fori_loop(0, R, body, 0)

    def deposit(nb, pairs):
        D[...] = jnp.zeros(D.shape, F32)

        def body(p, carry):
            f = p // (3 * X)
            t = p - 3 * X
            i = (1 - f) * (p // 3) + f * (t * (X - 1))
            a = (1 - f) * (p % 3) + f * 3
            xi = (1 - f) * (p // 3 + 1 + p % 3) + f * (t * (X + 3))
            lever = ((1 - f) * (p % 3 - 1) + f * (4 * t - 2)).astype(F32)
            for b in range(nb):
                acc = [[None] * 4 for _ in range(3)]
                for s in range(S):
                    q = i * S + s
                    wxy = PT[13 + a, q] * PT[17 + b, q]
                    wz = [PT[21 + c, q] for c in range(3)]
                    mw = PT[0, q] * wxy
                    base = []
                    slope = []
                    for k in range(3):
                        v = PT[1 + k, q] + lever * PT[4 + 3 * k, q]
                        if b == 0:
                            v = v - PT[5 + 3 * k, q]
                        elif b == 2:
                            v = v + PT[5 + 3 * k, q]
                        elif b == 3:
                            v = v + far_y * PT[5 + 3 * k, q]
                        base.append(v * wxy)
                        slope.append(PT[6 + 3 * k, q] * wxy)
                    for c in range(3):
                        terms = [mw * wz[c]]
                        for k in range(3):
                            v = base[k]
                            if c == 0:
                                v = v - slope[k]
                            elif c == 2:
                                v = v + slope[k]
                            terms.append(v * wz[c])
                        for n in range(4):
                            acc[c][n] = terms[n] if acc[c][n] is None else acc[c][n] + terms[n]
                for c in range(3):
                    for n in range(4):
                        D[b, c, n, xi] = D[b, c, n, xi] + acc[c][n]
            return carry

        lax.fori_loop(0, pairs, body, 0)

    def combine(step, nb, N):
        def body(x, carry):
            for n in range(4):
                for c in range(3):
                    GZ[c, n, x] = jnp.zeros((YE, Z), F32)
                    for b in range(3):
                        GZ[c, n, x, 1 + b : 1 + b + Y] = (
                            GZ[c, n, x, 1 + b : 1 + b + Y] + D[b, c, n, x]
                        )
                    if nb == 4:
                        GZ[c, n, x, 0:1] = GZ[c, n, x, 0:1] + D[3, c, n, x, 0:1]
                        GZ[c, n, x, YE - 1 : YE] = (
                            GZ[c, n, x, YE - 1 : YE] + D[3, c, n, x, Y - 1 : Y]
                        )
            return carry

        lax.fori_loop(0, XE, body, 0)
        pack = jnp.zeros((YE, Z), F32)
        for n in range(4):
            for x in range(XE):
                g0 = GZ[0, n, x]
                g2 = pltpu.roll(GZ[2, n, x], 1, 1)
                N[n, x] = (
                    GZ[1, n, x]
                    + jnp.where(lane < Z - 1, pltpu.roll(g0, Z - 1, 1), 0.0)
                    + jnp.where(lane > 0, g2, 0.0)
                )
                edge = jnp.where(is_low, g2, g0)
                l = n * XE + x
                moved = edge if l == 0 else pltpu.roll(edge, l, 1)
                pack = jnp.where(lane == l, moved, pack)
        PK[2 * step] = pack

    def unpack(value, l):
        return value if l == 0 else pltpu.roll(value, Z - l, 1)

    def velocities(step, N, SYH, SYL, RYL, RYH, RXL, RXH):
        nc = N.shape[0]
        nb = 3 if step == 0 else 4
        base = 6 * step
        if step == 0:
            N[4] = jnp.zeros((XE, YE, Z), F32)
            for x in range(X):
                N[4, x + 2, 2 : 2 + Y] = flags[x].astype(F32)
            pl.semaphore_wait(barrier, 9)
        copy = send(PK.at[2 * step], PKR.at[2 * step], base, sibling)
        copy.wait()
        got = PKR[2 * step]
        got = jnp.where(is_low, pltpu.roll(got, Z - 1, 1), got)
        at_edge = lane == jnp.where(is_low, Z - 1, 0)
        for n in range(4):
            for x in range(XE):
                N[n, x] = N[n, x] + jnp.where(at_edge, unpack(got, n * XE + x), 0.0)
        for n in range(nc):
            for x in range(XE):
                SYH[n, x] = N[n, x, Y : Y + 4]
                SYL[n, x] = N[n, x, 0:4]
        up = send(SYH, RYL, base + 1, at(0, 1))
        down = send(SYL, RYH, base + 2, at(0, -1))
        up.wait()
        down.wait()
        for n in range(nc):
            for x in range(XE):
                N[n, x, 0:4] = N[n, x, 0:4] + RYL[n, x]
                N[n, x, Y : Y + 4] = N[n, x, Y : Y + 4] + RYH[n, x]
        up = send(N.at[:, X : X + 4], RXL, base + 3, at(1, 0))
        down = send(N.at[:, 0:4], RXH, base + 4, at(-1, 0))
        up.wait()
        down.wait()
        pack = jnp.zeros((YE, Z), F32)
        for x in range(XE):
            tot = []
            for n in range(nc):
                v = N[n, x]
                if x < 4:
                    v = v + RXL[n, x]
                if x >= X:
                    v = v + RXH[n, x - X]
                tot.append(v)
            if step == 0:
                FL[x] = tot[4]
                fl = tot[4]
            else:
                fl = FL[x]
            inv = 1.0 / jnp.maximum(tot[0], MASS_FLOOR)
            for k in range(3):
                v = jnp.where(fl == 1.0, 0.0, tot[1 + k] * inv)
                if k == 2:
                    v = jnp.where(fl == 2.0, -PLATEN_SPEED, v)
                VZ[1, k, x] = v
                edge = jnp.where(is_low, pltpu.roll(v, 1, 1), v)
                l = k * XE + x
                moved = edge if l == 0 else pltpu.roll(edge, l, 1)
                pack = jnp.where(lane == l, moved, pack)
        PK[2 * step + 1] = pack
        copy = send(PK.at[2 * step + 1], PKR.at[2 * step + 1], base + 5, sibling)
        copy.wait()
        got = PKR[2 * step + 1]
        got = jnp.where(is_low, pltpu.roll(got, Z - 1, 1), got)
        got_high = jnp.where(is_low, got, 0.0)
        got_low = jnp.where(is_low, 0.0, got)
        if step == 0:
            VS[...] = jnp.zeros(VS.shape, F32)
        for k in range(3):
            for x in range(XE):
                l = k * XE + x
                v = VZ[1, k, x]
                VZ[0, k, x] = jnp.where(lane == 0, unpack(got_low, l), pltpu.roll(v, 1, 1))
                VZ[2, k, x] = jnp.where(
                    lane == Z - 1, unpack(got_high, l), pltpu.roll(v, Z - 1, 1)
                )

        def body(x, carry):
            for c in range(3):
                for k in range(3):
                    for b in range(3):
                        VS[b, c, k, x] = VZ[c, k, x, 1 + b : 1 + b + Y]
                    if nb == 4:
                        VS[3, c, k, x, 0:1] = VZ[c, k, x, 0:1]
                        VS[3, c, k, x, Y - 1 : Y] = VZ[c, k, x, YE - 1 : YE]
            return carry

        lax.fori_loop(0, XE, body, 0)

    def gather(step):
        nab = 3 if step == 0 else 4

        def body(q, carry):
            i = q // S
            s = q % S
            r = s * X + i
            side = i // (X - 1)
            wz = [PT[21 + c, q] for c in range(3)]
            wy = [PT[17 + b, q] for b in range(nab)]
            speed = [None] * 3
            mx = [None] * 3
            my = [None] * 3
            mz = [None] * 3

            def plus(total, term):
                return term if total is None else total + term

            for a in range(nab):
                xi = i + 1 + a if a < 3 else side * (X + 3)
                u = [None] * 3
                uy = [None] * 3
                uz = [None] * 3
                for b in range(nab):
                    for k in range(3):
                        low = wz[0] * VS[b, 0, k, xi]
                        mid = wz[1] * VS[b, 1, k, xi]
                        high = wz[2] * VS[b, 2, k, xi]
                        t = wy[b] * (low + mid + high)
                        u[k] = plus(u[k], t)
                        if b == 0:
                            uy[k] = -t
                        elif b == 2:
                            uy[k] = uy[k] + t
                        elif b == 3:
                            uy[k] = uy[k] + far_y * t
                        uz[k] = plus(uz[k], wy[b] * (high - low))
                wx = PT[13 + a, q]
                for k in range(3):
                    t = wx * u[k]
                    speed[k] = plus(speed[k], t)
                    if a == 0:
                        mx[k] = -t
                    elif a == 2:
                        mx[k] = mx[k] + t
                    elif a == 3:
                        mx[k] = mx[k] + (4 * side - 2).astype(F32) * t
                    my[k] = plus(my[k], wx * uy[k])
                    mz[k] = plus(mz[k], wx * uz[k])
            moments = [mx, my, mz]
            src = part if step == 0 else ST
            idx = r if step == 0 else q
            state = [src[c, idx] for c in range(22)]
            grad, div, stress = advance(state, speed, moments)
            if step == 0:
                for k in range(3):
                    ST[k, q] = state[k] + TIME_STEP * speed[k]
                    ST[3 + k, q] = speed[k]
                    for b in range(3):
                        ST[6 + 3 * k + b, q] = grad[k][b]
                for n in range(6):
                    ST[15 + n, q] = stress[n]
                ST[21, q] = state[21] * (1.0 + TIME_STEP * div)
            else:
                o = occ[r].astype(F32)
                stay = jnp.where(DM[q, 0:Y] < 0.5, o, 0.0)
                for n, v in enumerate(speed + stress):
                    out[n, r] = v * stay
                    VALS[n, q, 0:Y] = v * o
            return carry

        lax.fori_loop(0, R, body, 0)

    def direction_map():
        rows = lax.broadcasted_iota(jnp.int32, (R * 8, Z), 0)
        ks = lax.broadcasted_iota(jnp.int32, (Z, Z), 0)
        total = jnp.zeros((R * 8, Z), F32)
        for d in range(8):
            here = jnp.where(rows == rowq[d : d + 1, :], d + 1.0, 0.0).astype(jnp.bfloat16)
            hot = jnp.where(ks == kidx[d : d + 1, :], 1.0, 0.0).astype(jnp.bfloat16)
            total = total + lax.dot_general(
                here, hot, (((1,), (1,)), ((), ())), preferred_element_type=F32
            )
        DM[...] = total.reshape(R, 8, Z)

    def extract():
        ks = lax.broadcasted_iota(jnp.int32, (Z, Z), 0)
        copies = []
        for d in range(8):
            first, count = {-1: (0, S), 0: (0, R), 1: (R - S, S)}[SHIFT_X[d]]
            rows = lax.broadcasted_iota(jnp.int32, (count * 8, Z), 0) + first * 8
            here = rows == rowq[d : d + 1, :]
            hot = jnp.where(ks == kidx[d : d + 1, :], 1.0, 0.0).astype(jnp.bfloat16)
            for n in range(9):
                v = VALS[n, first : first + count].reshape(count * 8, Z)
                hi = v.astype(jnp.bfloat16)
                lo = (v - hi.astype(F32)).astype(jnp.bfloat16)
                t = jnp.dot(hi, hot, preferred_element_type=F32) + jnp.dot(
                    lo, hot, preferred_element_type=F32
                )
                RES[d, n : n + 1] = jnp.sum(jnp.where(here, t, 0.0), axis=0, keepdims=True)
            copies.append(
                send(RES.at[d], ARR.at[d], 12 + d, at(SHIFT_X[d], SHIFT_Y[d]))
            )
        for copy in copies:
            copy.wait()
        for d in range(8):
            arr[:, d] = ARR[d]

    prepare(0)
    deposit(3, 3 * X)
    combine(0, 3, N0)
    velocities(0, N0, SYH0, SYL0, RYL0, RYH0, RXL0, RXH0)
    direction_map()
    VALS[...] = jnp.zeros(VALS.shape, F32)
    gather(0)
    prepare(1)
    deposit(4, 3 * X + 2)
    combine(1, 4, N1)
    velocities(1, N1, SYH1, SYL1, RYL1, RYH1, RXL1, RXH1)
    gather(1)
    extract()


def body(n_gx, n_gy, particles, masses, occupied, node_flags, depart, arrive):
    _, S, X, Y, Z = particles.shape
    R, XE, YE = S * X, X + 4, Y + 4
    leaving = depart.reshape(8, Z)
    slot = leaving // (X * Y * Z)
    i = leaving // (Y * Z) % X
    j = leaving // Z % Y
    rowq = (i * S + slot) * 8 + j
    kidx = leaving % Z
    vmem = lambda *shape: pltpu.VMEM(shape, F32)
    final_state, arrivals = pl.pallas_call(
        functools.partial(kernel, S, X, Y, n_gx, n_gy),
        out_shape=(
            jax.ShapeDtypeStruct((9, R, Y, Z), F32),
            jax.ShapeDtypeStruct((9, 8, Z), F32),
        ),
        in_specs=[pl.BlockSpec(memory_space=pltpu.VMEM)] * 6,
        out_specs=(pl.BlockSpec(memory_space=pltpu.VMEM),) * 2,
        scratch_shapes=[
            vmem(22, R, Y, Z),
            vmem(24, R, Y, Z),
            vmem(4, 3, 4, XE, Y, Z),
            vmem(3, 4, XE, YE, Z),
            vmem(5, XE, YE, Z),
            vmem(4, XE, YE, Z),
            vmem(XE, YE, Z),
            vmem(3, 3, XE, YE, Z),
            vmem(4, 3, 3, XE, Y, Z),
            vmem(9, R, 8, Z),
            vmem(R, 8, Z),
            vmem(4, YE, Z),
            vmem(4, YE, Z),
            vmem(5, XE, 4, Z),
            vmem(5, XE, 4, Z),
            vmem(5, XE, 4, Z),
            vmem(5, XE, 4, Z),
            vmem(4, XE, 4, Z),
            vmem(4, XE, 4, Z),
            vmem(4, XE, 4, Z),
            vmem(4, XE, 4, Z),
            vmem(5, 4, YE, Z),
            vmem(5, 4, YE, Z),
            vmem(4, 4, YE, Z),
            vmem(4, 4, YE, Z),
            vmem(8, 9, Z),
            vmem(8, 9, Z),
            pltpu.SemaphoreType.DMA((20,)),
            pltpu.SemaphoreType.DMA((20,)),
        ],
        compiler_params=pltpu.CompilerParams(
            collective_id=0, has_side_effects=True, vmem_limit_bytes=60 * 1024 * 1024
        ),
        name="steps",
    )(
        particles.reshape(22, R, Y, Z),
        masses.reshape(R, Y, Z),
        occupied.reshape(R, Y, Z),
        node_flags,
        rowq,
        kidx,
    )
    return final_state.reshape(9, S, X, Y, Z), arrivals.reshape(9, 1, 1, 1, 8 * Z)


def solution(mesh):
    in_specs = (
        P(None, None, "gx", "gy", "col"),
        P(None, "gx", "gy", "col"),
        P(None, "gx", "gy", "col"),
        P("gx", "gy", "col"),
        P("gx", "gy", "col", None, None),
        P("gx", "gy", "col", None, None),
    )
    out_specs = (P(None, None, "gx", "gy", "col"), P(None, "gx", "gy", "col", None))
    sizes = mesh.shape
    assert sizes["col"] == 2
    return jax.shard_map(
        functools.partial(body, sizes["gx"], sizes["gy"]),
        mesh=mesh,
        in_specs=in_specs,
        out_specs=out_specs,
        check_vma=False,
    )
```

```python
import functools

import jax
import jax.numpy as jnp
from jax import lax
from jax.experimental import pallas as pl
from jax.experimental.pallas import tpu as pltpu
from jax.sharding import PartitionSpec as P

TIME_STEP = 0.2
LAME_FIRST = 2.5
SHEAR_MODULUS = 2.5
YIELD_STRESS = 1.2
MASS_FLOOR = 0.1
PLATEN_SPEED = 0.5
SHIFT_X = (-1, -1, -1, 0, 0, 1, 1, 1)
SHIFT_Y = (-1, 0, 1, -1, 1, -1, 0, 1)
STRESS_SLOT = ((0, 5, 4), (5, 1, 3), (4, 3, 2))
STRESS_PAIRS = ((0, 0), (1, 1), (2, 2), (1, 2), (0, 2), (0, 1))
F32 = jnp.float32


def spline(u):
    lo = 0.5 - u
    hi = 0.5 + u
    return (0.5 * lo * lo, 0.75 - u * u, 0.5 * hi * hi)


def advance(state, speed, moments):
    offset = state[0:3]
    grad = [[4.0 * (moments[b][k] - offset[b] * speed[k]) for b in range(3)] for k in range(3)]
    div = grad[0][0] + grad[1][1] + grad[2][2]
    trial = []
    for n in range(6):
        k, b = STRESS_PAIRS[n]
        if k == b:
            change = 2.0 * SHEAR_MODULUS * grad[k][k] + LAME_FIRST * div
        else:
            change = SHEAR_MODULUS * (grad[k][b] + grad[b][k])
        trial.append(state[15 + n] + TIME_STEP * change)
    pressure = (trial[0] + trial[1] + trial[2]) / 3.0
    dev = [trial[n] - pressure for n in range(3)] + trial[3:]
    square = (
        dev[0] * dev[0]
        + dev[1] * dev[1]
        + dev[2] * dev[2]
        + 2.0 * (dev[3] * dev[3] + dev[4] * dev[4] + dev[5] * dev[5])
    )
    factor = YIELD_STRESS / jnp.maximum(jnp.sqrt(1.5 * square), YIELD_STRESS)
    stress = [pressure + factor * dev[n] for n in range(3)] + [factor * dev[n] for n in range(3, 6)]
    return grad, div, stress


def kernel(
    S, X, Y, n_gx, n_gy,
    part, mass, occ, flags, depart,
    out, arr,
    ST, PT, D, GZ, N0, N1, FL, VZ, VS, VALS, DM,
    PK, PKR, SYH0, SYL0, RYL0, RYH0, SYH1, SYL1, RYL1, RYH1,
    RXL0, RXH0, RXL1, RXH1, NF, SFH, SFL, RFYL, RFYH, RFXL, RFXH, RES, ARR,
    send_sem, recv_sem,
):
    XE, YE = X + 4, Y + 4
    Z = 128
    R = S * X
    gx = lax.axis_index("gx")
    gy = lax.axis_index("gy")
    col = lax.axis_index("col")

    def at(dx, dy):
        return (lax.rem(gx + dx + n_gx, n_gx), lax.rem(gy + dy + n_gy, n_gy), col)

    sibling = (gx, gy, 1 - col)

    barrier = pltpu.get_barrier_semaphore()
    for dx, dy in zip(SHIFT_X, SHIFT_Y):
        pl.semaphore_signal(
            barrier, inc=1, device_id=at(dx, dy), device_id_type=pl.DeviceIdType.MESH
        )
    pl.semaphore_signal(barrier, inc=1, device_id=sibling, device_id_type=pl.DeviceIdType.MESH)

    def send(src, dst, slot, target):
        copy = pltpu.make_async_remote_copy(
            src_ref=src,
            dst_ref=dst,
            send_sem=send_sem.at[slot],
            recv_sem=recv_sem.at[slot],
            device_id=target,
            device_id_type=pl.DeviceIdType.MESH,
        )
        copy.start()
        return copy

    lane = lax.broadcasted_iota(jnp.int32, (YE, Z), 1)
    is_low = (lane * 0 + col) == 0
    row = lax.broadcasted_iota(jnp.int32, (Y, Z), 0)
    far_y = jnp.where(row == 0, -2.0, 2.0).astype(F32)

    def prepare(step):
        def body(q, carry):
            i = q // S
            s = q % S
            if step == 0:
                st = [part[c, s, pl.ds(i, Y, stride=X), :] for c in range(22)]
            else:
                st = [ST[c, q] for c in range(22)]
            o = occ[s, pl.ds(i, Y, stride=X), :].astype(F32)
            m = mass[s, pl.ds(i, Y, stride=X), :] * o
            w = (4.0 * TIME_STEP) * (st[21] * o)
            ws = [w * st[15 + n] for n in range(6)]
            Q = [[m * st[6 + 3 * k + b] - ws[STRESS_SLOT[k][b]] for b in range(3)] for k in range(3)]
            anchor = [
                m * st[3 + k] - (Q[k][0] * st[0] + Q[k][1] * st[1] + Q[k][2] * st[2])
                for k in range(3)
            ]
            PT[0, q] = m
            for k in range(3):
                PT[1 + k, q] = anchor[k]
                for b in range(3):
                    PT[4 + 3 * k + b, q] = Q[k][b]
            if step == 0:
                for dim, base in ((0, 13), (1, 17)):
                    ws3 = spline(st[dim])
                    for e in range(3):
                        PT[base + e, q] = ws3[e]
            else:
                code = DM[q, 0:Y]
                zero = jnp.zeros_like(code)
                sx = jnp.where(code < 3.5, -1.0, jnp.where(code > 5.5, 1.0, 0.0))
                sx = jnp.where(code < 0.5, 0.0, sx)
                low_y = (code == 1.0) | (code == 4.0) | (code == 6.0)
                high_y = (code == 3.0) | (code == 5.0) | (code == 8.0)
                sy = jnp.where(low_y, -1.0, jnp.where(high_y, 1.0, 0.0))
                for dim, base, sh in ((0, 13, sx), (1, 17, sy)):
                    p0, p1, p2 = spline(st[dim] - sh)
                    up = sh > 0.5
                    down = sh < -0.5
                    PT[base, q] = jnp.where(up, zero, jnp.where(down, p1, p0))
                    PT[base + 1, q] = jnp.where(up, p0, jnp.where(down, p2, p1))
                    PT[base + 2, q] = jnp.where(up, p1, jnp.where(down, zero, p2))
                    PT[base + 3, q] = jnp.where(up, p2, jnp.where(down, p0, zero))
            wz = spline(st[2])
            for e in range(3):
                PT[21 + e, q] = wz[e]
            return carry

        lax.fori_loop(0, R, body, 0)

    def deposit(nb, pairs):
        D[...] = jnp.zeros(D.shape, F32)

        def body(p, carry):
            f = p // (3 * X)
            t = p - 3 * X
            i = (1 - f) * (p // 3) + f * (t * (X - 1))
            a = (1 - f) * (p % 3) + f * 3
            xi = (1 - f) * (p // 3 + 1 + p % 3) + f * (t * (X + 3))
            lever = ((1 - f) * (p % 3 - 1) + f * (4 * t - 2)).astype(F32)
            for b in range(nb):
                acc = [[None] * 4 for _ in range(3)]
                for s in range(S):
                    q = i * S + s
                    wxy = PT[13 + a, q] * PT[17 + b, q]
                    wz = [PT[21 + c, q] for c in range(3)]
                    mw = PT[0, q] * wxy
                    base = []
                    slope = []
                    for k in range(3):
                        v = PT[1 + k, q] + lever * PT[4 + 3 * k, q]
                        if b == 0:
                            v = v - PT[5 + 3 * k, q]
                        elif b == 2:
                            v = v + PT[5 + 3 * k, q]
                        elif b == 3:
                            v = v + far_y * PT[5 + 3 * k, q]
                        base.append(v * wxy)
                        slope.append(PT[6 + 3 * k, q] * wxy)
                    for c in range(3):
                        terms = [mw * wz[c]]
                        for k in range(3):
                            v = base[k]
                            if c == 0:
                                v = v - slope[k]
                            elif c == 2:
                                v = v + slope[k]
                            terms.append(v * wz[c])
                        for n in range(4):
                            acc[c][n] = terms[n] if acc[c][n] is None else acc[c][n] + terms[n]
                for c in range(3):
                    for n in range(4):
                        D[b, c, n, xi] = D[b, c, n, xi] + acc[c][n]
            return carry

        lax.fori_loop(0, pairs, body, 0)

    def combine(step, nb, N):
        def body(x, carry):
            for n in range(4):
                for c in range(3):
                    GZ[c, n, x] = jnp.zeros((YE, Z), F32)
                    for b in range(3):
                        GZ[c, n, x, 1 + b : 1 + b + Y] = (
                            GZ[c, n, x, 1 + b : 1 + b + Y] + D[b, c, n, x]
                        )
                    if nb == 4:
                        GZ[c, n, x, 0:1] = GZ[c, n, x, 0:1] + D[3, c, n, x, 0:1]
                        GZ[c, n, x, YE - 1 : YE] = (
                            GZ[c, n, x, YE - 1 : YE] + D[3, c, n, x, Y - 1 : Y]
                        )
            return carry

        h = 1 + step
        lax.fori_loop(2 - h, X + 2 + h, body, 0)
        pack = jnp.zeros((YE, Z), F32)
        for n in range(4):
            for x in range(2 - h, X + 2 + h):
                g0 = GZ[0, n, x]
                g2 = pltpu.roll(GZ[2, n, x], 1, 1)
                N[n, x] = (
                    GZ[1, n, x]
                    + jnp.where(lane < Z - 1, pltpu.roll(g0, Z - 1, 1), 0.0)
                    + jnp.where(lane > 0, g2, 0.0)
                )
                edge = jnp.where(is_low, g2, g0)
                l = n * XE + x
                moved = edge if l == 0 else pltpu.roll(edge, l, 1)
                pack = jnp.where(lane == l, moved, pack)
        PK[2 * step] = pack

    def unpack(value, l):
        return value if l == 0 else pltpu.roll(value, Z - l, 1)

    def velocities(step, N, SYH, SYL, RYL, RYH, RXL, RXH):
        h = 1 + step
        lo = 2 - h
        xs = range(lo, X + 2 + h)
        nb = 3 if step == 0 else 4
        base = 6 * step
        flag_copies = []
        if step == 0:
            NF[...] = jnp.zeros(NF.shape, F32)
            for x in range(X):
                fl = flags[pl.ds(x, Y, stride=X), :].astype(F32)
                NF[x + 2, 2 : 2 + Y] = fl
                SFH[x] = jnp.concatenate([fl[Y - 2 : Y], jnp.zeros((2, Z), F32)], axis=0)
                SFL[x] = jnp.concatenate([jnp.zeros((2, Z), F32), fl[0:2]], axis=0)
            pl.semaphore_wait(barrier, 9)
            flag_copies = [send(SFH, RFYL, 20, at(0, 1)), send(SFL, RFYH, 21, at(0, -1))]
        copy = send(PK.at[2 * step], PKR.at[2 * step], base, sibling)
        copy.wait()
        got = PKR[2 * step]
        got = jnp.where(is_low, pltpu.roll(got, Z - 1, 1), got)
        at_edge = lane == jnp.where(is_low, Z - 1, 0)
        for n in range(4):
            for x in xs:
                v = N[n, x] + jnp.where(at_edge, unpack(got, n * XE + x), 0.0)
                N[n, x] = v
                SYH[n, x - lo] = v[Y + lo : Y + lo + 2 * h]
                SYL[n, x - lo] = v[lo : lo + 2 * h]
        up = send(SYH, RYL, base + 1, at(0, 1))
        down = send(SYL, RYH, base + 2, at(0, -1))
        for copy in flag_copies:
            copy.wait()
        flag_copies = []
        if step == 0:
            for x in range(X):
                NF[x + 2, 0:4] = NF[x + 2, 0:4] + RFYL[x]
                NF[x + 2, Y : Y + 4] = NF[x + 2, Y : Y + 4] + RFYH[x]
            flag_copies = [
                send(NF.at[X : X + 4], RFXL, 22, at(1, 0)),
                send(NF.at[0:4], RFXH, 23, at(-1, 0)),
            ]
        up.wait()
        down.wait()
        for n in range(4):
            for x in xs:
                N[n, x, lo : lo + 2 * h] = N[n, x, lo : lo + 2 * h] + RYL[n, x - lo]
                N[n, x, Y + lo : Y + lo + 2 * h] = (
                    N[n, x, Y + lo : Y + lo + 2 * h] + RYH[n, x - lo]
                )
        up = send(N.at[:, X + lo : X + lo + 2 * h], RXL, base + 3, at(1, 0))
        down = send(N.at[:, lo : lo + 2 * h], RXH, base + 4, at(-1, 0))
        for copy in flag_copies:
            copy.wait()
        if step == 0:
            for x in range(XE):
                v = NF[x]
                if x < 4:
                    v = v + RFXL[x]
                if x >= X:
                    v = v + RFXH[x - X]
                FL[x] = v
        up.wait()
        down.wait()
        pack = jnp.zeros((YE, Z), F32)
        for x in xs:
            tot = []
            for n in range(4):
                v = N[n, x]
                if x < lo + 2 * h:
                    v = v + RXL[n, x - lo]
                if x >= X + lo:
                    v = v + RXH[n, x - X - lo]
                tot.append(v)
            fl = FL[x]
            inv = 1.0 / jnp.maximum(tot[0], MASS_FLOOR)
            for k in range(3):
                v = jnp.where(fl == 1.0, 0.0, tot[1 + k] * inv)
                if k == 2:
                    v = jnp.where(fl == 2.0, -PLATEN_SPEED, v)
                VZ[1, k, x] = v
                edge = jnp.where(is_low, pltpu.roll(v, 1, 1), v)
                l = k * XE + x
                moved = edge if l == 0 else pltpu.roll(edge, l, 1)
                pack = jnp.where(lane == l, moved, pack)
        PK[2 * step + 1] = pack
        copy = send(PK.at[2 * step + 1], PKR.at[2 * step + 1], base + 5, sibling)
        copy.wait()
        got = PKR[2 * step + 1]
        got = jnp.where(is_low, pltpu.roll(got, Z - 1, 1), got)
        got_high = jnp.where(is_low, got, 0.0)
        got_low = jnp.where(is_low, 0.0, got)
        if step == 0:
            VS[...] = jnp.zeros(VS.shape, F32)
        for k in range(3):
            for x in xs:
                l = k * XE + x
                v = VZ[1, k, x]
                VZ[0, k, x] = jnp.where(lane == 0, unpack(got_low, l), pltpu.roll(v, 1, 1))
                VZ[2, k, x] = jnp.where(
                    lane == Z - 1, unpack(got_high, l), pltpu.roll(v, Z - 1, 1)
                )

        def body(x, carry):
            for c in range(3):
                for k in range(3):
                    for b in range(3):
                        VS[b, c, k, x] = VZ[c, k, x, 1 + b : 1 + b + Y]
                    if nb == 4:
                        VS[3, c, k, x, 0:1] = VZ[c, k, x, 0:1]
                        VS[3, c, k, x, Y - 1 : Y] = VZ[c, k, x, YE - 1 : YE]
            return carry

        lax.fori_loop(lo, X + 2 + h, body, 0)

    def gather(step):
        nab = 3 if step == 0 else 4

        def body(na, q, carry):
            i = q // S
            s = q % S
            side = i // (X - 1)
            wz = [PT[21 + c, q] for c in range(3)]
            wy = [PT[17 + b, q] for b in range(nab)]
            speed = [None] * 3
            mx = [None] * 3
            my = [None] * 3
            mz = [None] * 3

            def plus(total, term):
                return term if total is None else total + term

            for a in range(na):
                xi = i + 1 + a if a < 3 else side * (X + 3)
                u = [None] * 3
                uy = [None] * 3
                uz = [None] * 3
                for b in range(nab):
                    for k in range(3):
                        low = wz[0] * VS[b, 0, k, xi]
                        mid = wz[1] * VS[b, 1, k, xi]
                        high = wz[2] * VS[b, 2, k, xi]
                        t = wy[b] * (low + mid + high)
                        u[k] = plus(u[k], t)
                        if b == 0:
                            uy[k] = -t
                        elif b == 2:
                            uy[k] = uy[k] + t
                        elif b == 3:
                            uy[k] = uy[k] + far_y * t
                        uz[k] = plus(uz[k], wy[b] * (high - low))
                wx = PT[13 + a, q]
                for k in range(3):
                    t = wx * u[k]
                    speed[k] = plus(speed[k], t)
                    if a == 0:
                        mx[k] = -t
                    elif a == 2:
                        mx[k] = mx[k] + t
                    elif a == 3:
                        mx[k] = mx[k] + (4 * side - 2).astype(F32) * t
                    my[k] = plus(my[k], wx * uy[k])
                    mz[k] = plus(mz[k], wx * uz[k])
            moments = [mx, my, mz]
            if step == 0:
                state = [part[c, s, pl.ds(i, Y, stride=X), :] for c in range(22)]
            else:
                state = [ST[c, q] for c in range(22)]
            grad, div, stress = advance(state, speed, moments)
            if step == 0:
                for k in range(3):
                    ST[k, q] = state[k] + TIME_STEP * speed[k]
                    ST[3 + k, q] = speed[k]
                    for b in range(3):
                        ST[6 + 3 * k + b, q] = grad[k][b]
                for n in range(6):
                    ST[15 + n, q] = stress[n]
                ST[21, q] = state[21] * (1.0 + TIME_STEP * div)
            else:
                o = occ[s, pl.ds(i, Y, stride=X), :].astype(F32)
                stay = jnp.where(DM[q, 0:Y] < 0.5, o, 0.0)
                for n, v in enumerate(speed + stress):
                    out[n, s, pl.ds(i, Y, stride=X), :] = v * stay
                    VALS[n, q, 0:Y] = v * o
            return carry

        if step == 0:
            lax.fori_loop(0, R, functools.partial(body, 3), 0)
        else:
            edge_body = lambda t, carry: body(4, t + (t // S) * (R - 2 * S), carry)
            lax.fori_loop(0, 2 * S, edge_body, 0)
            lax.fori_loop(S, R - S, functools.partial(body, 3), 0)

    ident = depart[...].astype(F32)
    line = jnp.floor((ident + 0.5) * (1.0 / Z))
    kidx = ident - line * Z
    slot = jnp.floor((line + 0.5) * (1.0 / (X * Y)))
    cell = line - slot * (X * Y)
    cell_x = jnp.floor((cell + 0.5) * (1.0 / Y))
    rowq = (cell_x * S + slot) * 8.0 + (cell - cell_x * Y)

    def direction_map():
        rows = lax.broadcasted_iota(jnp.int32, (R * 8, Z), 0).astype(F32)
        ks = lax.broadcasted_iota(jnp.int32, (Z, Z), 0).astype(F32)
        total = jnp.zeros((R * 8, Z), F32)
        for d in range(8):
            here = jnp.where(rows == rowq[d : d + 1, :], d + 1.0, 0.0).astype(jnp.bfloat16)
            hot = jnp.where(ks == kidx[d : d + 1, :], 1.0, 0.0).astype(jnp.bfloat16)
            total = total + lax.dot_general(
                here, hot, (((1,), (1,)), ((), ())), preferred_element_type=F32
            )
        DM[...] = total.reshape(R, 8, Z)

    def extract():
        ks = lax.broadcasted_iota(jnp.int32, (Z, Z), 0).astype(F32)
        copies = []
        for first, count, ds in ((0, S, (0, 1, 2)), (R - S, S, (5, 6, 7)), (0, R, (3, 4))):
            rows = lax.broadcasted_iota(jnp.int32, (count * 8, Z), 0).astype(F32) + first * 8.0
            hot = jnp.concatenate(
                [jnp.where(ks == kidx[d : d + 1, :], 1.0, 0.0) for d in ds], axis=1
            ).astype(jnp.bfloat16)
            hot = jnp.concatenate([hot, hot], axis=0)
            for n in range(9):
                v = VALS[n, first : first + count].reshape(count * 8, Z)
                hi = v.astype(jnp.bfloat16)
                low = (v - hi.astype(F32)).astype(jnp.bfloat16)
                t = jnp.dot(
                    jnp.concatenate([hi, low], axis=1), hot, preferred_element_type=F32
                )
                for e, d in enumerate(ds):
                    here = rows == rowq[d : d + 1, :]
                    RES[d, n : n + 1] = jnp.sum(
                        jnp.where(here, t[:, e * Z : (e + 1) * Z], 0.0), axis=0, keepdims=True
                    )
            for d in ds:
                copies.append(
                    send(RES.at[d], ARR.at[d], 12 + d, at(SHIFT_X[d], SHIFT_Y[d]))
                )
        for copy in copies:
            copy.wait()
        for d in range(8):
            arr[:, d] = ARR[d]

    prepare(0)
    deposit(3, 3 * X)
    combine(0, 3, N0)
    velocities(0, N0, SYH0, SYL0, RYL0, RYH0, RXL0, RXH0)
    direction_map()
    VALS[...] = jnp.zeros(VALS.shape, F32)
    gather(0)
    prepare(1)
    deposit(4, 3 * X + 2)
    combine(1, 4, N1)
    velocities(1, N1, SYH1, SYL1, RYL1, RYH1, RXL1, RXH1)
    gather(1)
    extract()


def body(n_gx, n_gy, particles, masses, occupied, node_flags, depart, arrive):
    _, S, X, Y, Z = particles.shape
    R, XE, YE = S * X, X + 4, Y + 4
    vmem = lambda *shape: pltpu.VMEM(shape, F32)
    final_state, arrivals = pl.pallas_call(
        functools.partial(kernel, S, X, Y, n_gx, n_gy),
        out_shape=(
            jax.ShapeDtypeStruct((9, S, Y * X, Z), F32),
            jax.ShapeDtypeStruct((9, 8, Z), F32),
        ),
        in_specs=[pl.BlockSpec(memory_space=pltpu.VMEM)] * 5,
        out_specs=(pl.BlockSpec(memory_space=pltpu.VMEM),) * 2,
        scratch_shapes=[
            vmem(22, R, Y, Z),
            vmem(24, R, Y, Z),
            vmem(4, 3, 4, XE, Y, Z),
            vmem(3, 4, XE, YE, Z),
            vmem(4, XE, YE, Z),
            vmem(4, XE, YE, Z),
            vmem(XE, YE, Z),
            vmem(3, 3, XE, YE, Z),
            vmem(4, 3, 3, XE, Y, Z),
            vmem(9, R, 8, Z),
            vmem(R, 8, Z),
            vmem(4, YE, Z),
            vmem(4, YE, Z),
            vmem(4, X + 2, 2, Z),
            vmem(4, X + 2, 2, Z),
            vmem(4, X + 2, 2, Z),
            vmem(4, X + 2, 2, Z),
            vmem(4, XE, 4, Z),
            vmem(4, XE, 4, Z),
            vmem(4, XE, 4, Z),
            vmem(4, XE, 4, Z),
            vmem(4, 2, YE, Z),
            vmem(4, 2, YE, Z),
            vmem(4, 4, YE, Z),
            vmem(4, 4, YE, Z),
            vmem(XE, YE, Z),
            vmem(X, 4, Z),
            vmem(X, 4, Z),
            vmem(X, 4, Z),
            vmem(X, 4, Z),
            vmem(4, YE, Z),
            vmem(4, YE, Z),
            vmem(8, 9, Z),
            vmem(8, 9, Z),
            pltpu.SemaphoreType.DMA((24,)),
            pltpu.SemaphoreType.DMA((24,)),
        ],
        compiler_params=pltpu.CompilerParams(
            collective_id=0, has_side_effects=True, vmem_limit_bytes=60 * 1024 * 1024
        ),
        name="steps",
    )(
        particles.transpose(0, 1, 3, 2, 4).reshape(22, S, Y * X, Z),
        masses.transpose(0, 2, 1, 3).reshape(S, Y * X, Z),
        occupied.transpose(0, 2, 1, 3).reshape(S, Y * X, Z),
        node_flags.transpose(1, 0, 2).reshape(Y * X, Z),
        depart.reshape(8, Z),
    )
    final_state = final_state.reshape(9, S, Y, X, Z).transpose(0, 1, 3, 2, 4)
    return final_state, arrivals.reshape(9, 1, 1, 1, 8 * Z)


def solution(mesh):
    in_specs = (
        P(None, None, "gx", "gy", "col"),
        P(None, "gx", "gy", "col"),
        P(None, "gx", "gy", "col"),
        P("gx", "gy", "col"),
        P("gx", "gy", "col", None, None),
        P("gx", "gy", "col", None, None),
    )
    out_specs = (P(None, None, "gx", "gy", "col"), P(None, "gx", "gy", "col", None))
    sizes = mesh.shape
    assert sizes["col"] == 2
    return jax.shard_map(
        functools.partial(body, sizes["gx"], sizes["gy"]),
        mesh=mesh,
        in_specs=in_specs,
        out_specs=out_specs,
        check_vma=False,
    )
```

```python
import functools

import jax
import jax.numpy as jnp
from jax import lax
from jax.experimental import pallas as pl
from jax.experimental.pallas import tpu as pltpu
from jax.sharding import PartitionSpec as P

TIME_STEP = 0.2
LAME_FIRST = 2.5
SHEAR_MODULUS = 2.5
YIELD_STRESS = 1.2
MASS_FLOOR = 0.1
PLATEN_SPEED = 0.5
SHIFT_X = (-1, -1, -1, 0, 0, 1, 1, 1)
SHIFT_Y = (-1, 0, 1, -1, 1, -1, 0, 1)
STRESS_SLOT = ((0, 5, 4), (5, 1, 3), (4, 3, 2))
STRESS_PAIRS = ((0, 0), (1, 1), (2, 2), (1, 2), (0, 2), (0, 1))
F32 = jnp.float32


def spline(u):
    lo = 0.5 - u
    hi = 0.5 + u
    return (0.5 * lo * lo, 0.75 - u * u, 0.5 * hi * hi)


def advance(state, speed, moments):
    offset = state[0:3]
    grad = [[4.0 * (moments[b][k] - offset[b] * speed[k]) for b in range(3)] for k in range(3)]
    div = grad[0][0] + grad[1][1] + grad[2][2]
    trial = []
    for n in range(6):
        k, b = STRESS_PAIRS[n]
        if k == b:
            change = 2.0 * SHEAR_MODULUS * grad[k][k] + LAME_FIRST * div
        else:
            change = SHEAR_MODULUS * (grad[k][b] + grad[b][k])
        trial.append(state[15 + n] + TIME_STEP * change)
    pressure = (trial[0] + trial[1] + trial[2]) / 3.0
    dev = [trial[n] - pressure for n in range(3)] + trial[3:]
    square = (
        dev[0] * dev[0]
        + dev[1] * dev[1]
        + dev[2] * dev[2]
        + 2.0 * (dev[3] * dev[3] + dev[4] * dev[4] + dev[5] * dev[5])
    )
    factor = YIELD_STRESS / jnp.maximum(jnp.sqrt(1.5 * square), YIELD_STRESS)
    stress = [pressure + factor * dev[n] for n in range(3)] + [factor * dev[n] for n in range(3, 6)]
    return grad, div, stress


def kernel(
    S, X, Y, n_gx, n_gy,
    part, mass, occ, flags, depart,
    out, arr,
    ST, PT, D, GZ, N0, N1, FL, VZ, VS, VALS, DM,
    PK, PKR, SYH0, SYL0, RYL0, RYH0, SYH1, SYL1, RYL1, RYH1,
    RXL0, RXH0, RXL1, RXH1, RC0, RC1, FB, RF, RES, ARR,
    send_sem, recv_sem,
):
    XE, YE = X + 4, Y + 4
    Z = 128
    R = S * X
    gx = lax.axis_index("gx")
    gy = lax.axis_index("gy")
    col = lax.axis_index("col")

    def at(dx, dy):
        return (lax.rem(gx + dx + n_gx, n_gx), lax.rem(gy + dy + n_gy, n_gy), col)

    sibling = (gx, gy, 1 - col)

    barrier = pltpu.get_barrier_semaphore()
    for dx, dy in zip(SHIFT_X, SHIFT_Y):
        pl.semaphore_signal(
            barrier, inc=1, device_id=at(dx, dy), device_id_type=pl.DeviceIdType.MESH
        )
    pl.semaphore_signal(barrier, inc=1, device_id=sibling, device_id_type=pl.DeviceIdType.MESH)

    def send(src, dst, slot, target):
        copy = pltpu.make_async_remote_copy(
            src_ref=src,
            dst_ref=dst,
            send_sem=send_sem.at[slot],
            recv_sem=recv_sem.at[slot],
            device_id=target,
            device_id_type=pl.DeviceIdType.MESH,
        )
        copy.start()
        return copy

    lane = lax.broadcasted_iota(jnp.int32, (YE, Z), 1)
    is_low = (lane * 0 + col) == 0
    row = lax.broadcasted_iota(jnp.int32, (Y, Z), 0)
    far_y = jnp.where(row == 0, -2.0, 2.0).astype(F32)

    def prepare(step):
        def body(q, carry):
            i = q // S
            s = q % S
            if step == 0:
                st = [part[c, s, pl.ds(i, Y, stride=X), :] for c in range(22)]
            else:
                st = [ST[c, q] for c in range(22)]
            o = occ[s, pl.ds(i, Y, stride=X), :].astype(F32)
            m = mass[s, pl.ds(i, Y, stride=X), :] * o
            w = (4.0 * TIME_STEP) * (st[21] * o)
            ws = [w * st[15 + n] for n in range(6)]
            Q = [[m * st[6 + 3 * k + b] - ws[STRESS_SLOT[k][b]] for b in range(3)] for k in range(3)]
            anchor = [
                m * st[3 + k] - (Q[k][0] * st[0] + Q[k][1] * st[1] + Q[k][2] * st[2])
                for k in range(3)
            ]
            PT[0, q] = m
            for k in range(3):
                PT[1 + k, q] = anchor[k]
                for b in range(3):
                    PT[4 + 3 * k + b, q] = Q[k][b]
            if step == 0:
                for dim, base in ((0, 13), (1, 17)):
                    ws3 = spline(st[dim])
                    for e in range(3):
                        PT[base + e, q] = ws3[e]
            else:
                code = DM[q, 0:Y]
                zero = jnp.zeros_like(code)
                sx = jnp.where(code < 3.5, -1.0, jnp.where(code > 5.5, 1.0, 0.0))
                sx = jnp.where(code < 0.5, 0.0, sx)
                low_y = (code == 1.0) | (code == 4.0) | (code == 6.0)
                high_y = (code == 3.0) | (code == 5.0) | (code == 8.0)
                sy = jnp.where(low_y, -1.0, jnp.where(high_y, 1.0, 0.0))
                for dim, base, sh in ((0, 13, sx), (1, 17, sy)):
                    p0, p1, p2 = spline(st[dim] - sh)
                    up = sh > 0.5
                    down = sh < -0.5
                    PT[base, q] = jnp.where(up, zero, jnp.where(down, p1, p0))
                    PT[base + 1, q] = jnp.where(up, p0, jnp.where(down, p2, p1))
                    PT[base + 2, q] = jnp.where(up, p1, jnp.where(down, zero, p2))
                    PT[base + 3, q] = jnp.where(up, p2, jnp.where(down, p0, zero))
            wz = spline(st[2])
            for e in range(3):
                PT[21 + e, q] = wz[e]
            return carry

        lax.fori_loop(0, R, body, 0)

    def deposit(nb, pairs):
        def body(p, carry):
            f = p // (3 * X)
            t = p - 3 * X
            i = (1 - f) * (p // 3) + f * (t * (X - 1))
            a = (1 - f) * (p % 3) + f * 3
            xi = (1 - f) * (p // 3 + 1 + p % 3) + f * (t * (X + 3))
            lever = ((1 - f) * (p % 3 - 1) + f * (4 * t - 2)).astype(F32)
            for b in range(nb):
                acc = [[None] * 4 for _ in range(3)]
                for s in range(S):
                    q = i * S + s
                    wxy = PT[13 + a, q] * PT[17 + b, q]
                    wz = [PT[21 + c, q] for c in range(3)]
                    mw = PT[0, q] * wxy
                    base = []
                    slope = []
                    for k in range(3):
                        v = PT[1 + k, q] + lever * PT[4 + 3 * k, q]
                        if b == 0:
                            v = v - PT[5 + 3 * k, q]
                        elif b == 2:
                            v = v + PT[5 + 3 * k, q]
                        elif b == 3:
                            v = v + far_y * PT[5 + 3 * k, q]
                        base.append(v * wxy)
                        slope.append(PT[6 + 3 * k, q] * wxy)
                    for c in range(3):
                        terms = [mw * wz[c]]
                        for k in range(3):
                            v = base[k]
                            if c == 0:
                                v = v - slope[k]
                            elif c == 2:
                                v = v + slope[k]
                            terms.append(v * wz[c])
                        for n in range(4):
                            acc[c][n] = terms[n] if acc[c][n] is None else acc[c][n] + terms[n]
                for c in range(3):
                    for n in range(4):
                        D[b, c, n, xi] = D[b, c, n, xi] + acc[c][n]
            return carry

        lax.fori_loop(0, pairs, body, 0)

    def combine(step, nb, N):
        def body(x, carry):
            for n in range(4):
                for c in range(3):
                    GZ[c, n, x] = jnp.zeros((YE, Z), F32)
                    for b in range(3):
                        GZ[c, n, x, 1 + b : 1 + b + Y] = (
                            GZ[c, n, x, 1 + b : 1 + b + Y] + D[b, c, n, x]
                        )
                    if nb == 4:
                        GZ[c, n, x, 0:1] = GZ[c, n, x, 0:1] + D[3, c, n, x, 0:1]
                        GZ[c, n, x, YE - 1 : YE] = (
                            GZ[c, n, x, YE - 1 : YE] + D[3, c, n, x, Y - 1 : Y]
                        )
            return carry

        h = 1 + step
        lax.fori_loop(2 - h, X + 2 + h, body, 0)
        pack = jnp.zeros((YE, Z), F32)
        for n in range(4):
            for x in range(2 - h, X + 2 + h):
                g0 = GZ[0, n, x]
                g2 = pltpu.roll(GZ[2, n, x], 1, 1)
                N[n, x] = (
                    GZ[1, n, x]
                    + jnp.where(lane < Z - 1, pltpu.roll(g0, Z - 1, 1), 0.0)
                    + jnp.where(lane > 0, g2, 0.0)
                )
                edge = jnp.where(is_low, g2, g0)
                l = n * XE + x
                moved = edge if l == 0 else pltpu.roll(edge, l, 1)
                pack = jnp.where(lane == l, moved, pack)
        PK[2 * step] = pack

    def unpack(value, l):
        return value if l == 0 else pltpu.roll(value, Z - l, 1)

    ident = depart[...].astype(F32)
    line = jnp.floor((ident + 0.5) * (1.0 / Z))
    kidx = ident - line * Z
    slot = jnp.floor((line + 0.5) * (1.0 / (X * Y)))
    cell = line - slot * (X * Y)
    cell_x = jnp.floor((cell + 0.5) * (1.0 / Y))
    rowq = (cell_x * S + slot) * 8.0 + (cell - cell_x * Y)

    def direction_map():
        rows = lax.broadcasted_iota(jnp.int32, (R * 8, Z), 0).astype(F32)
        ks = lax.broadcasted_iota(jnp.int32, (Z, Z), 0).astype(F32)
        total = jnp.zeros((R * 8, Z), F32)
        for d in range(8):
            here = jnp.where(rows == rowq[d : d + 1, :], d + 1.0, 0.0).astype(jnp.bfloat16)
            hot = jnp.where(ks == kidx[d : d + 1, :], 1.0, 0.0).astype(jnp.bfloat16)
            total = total + lax.dot_general(
                here, hot, (((1,), (1,)), ((), ())), preferred_element_type=F32
            )
        DM[...] = total.reshape(R, 8, Z)

    def velocities(step, N, SYH, SYL, RYL, RYH, RXL, RXH, RC):
        h = 1 + step
        lo = 2 - h
        xs = range(lo, X + 2 + h)
        nb = 3 if step == 0 else 4
        base = 10 * step
        flag_copies = []
        if step == 0:
            for x in range(X):
                fl = flags[pl.ds(x, Y, stride=X), :].astype(F32)
                FB[x] = fl
                FL[x + 2, 2 : 2 + Y] = fl
            pl.semaphore_wait(barrier, 9)
        copy = send(PK.at[2 * step], PKR.at[2 * step], base, sibling)
        if step == 0:
            for d in range(8):
                flag_copies.append(send(FB, RF.at[d], 28 + d, at(SHIFT_X[d], SHIFT_Y[d])))
            direction_map()
        copy.wait()
        got = PKR[2 * step]
        got = jnp.where(is_low, pltpu.roll(got, Z - 1, 1), got)
        at_edge = lane == jnp.where(is_low, Z - 1, 0)
        for n in range(4):
            for x in xs:
                v = N[n, x] + jnp.where(at_edge, unpack(got, n * XE + x), 0.0)
                N[n, x] = v
                SYH[n, x - lo] = v[Y + lo : Y + lo + 2 * h]
                SYL[n, x - lo] = v[lo : lo + 2 * h]
        w = 2 * h
        copies = [
            send(N.at[:, X + lo : X + lo + w], RXL, base + 1, at(1, 0)),
            send(N.at[:, lo : lo + w], RXH, base + 2, at(-1, 0)),
            send(SYH, RYL, base + 3, at(0, 1)),
            send(SYL, RYH, base + 4, at(0, -1)),
            send(SYH.at[:, X : X + w], RC.at[0], base + 5, at(1, 1)),
            send(SYH.at[:, 0:w], RC.at[1], base + 6, at(-1, 1)),
            send(SYL.at[:, X : X + w], RC.at[2], base + 7, at(1, -1)),
            send(SYL.at[:, 0:w], RC.at[3], base + 8, at(-1, -1)),
        ]
        if step == 0:
            VALS[...] = jnp.zeros(VALS.shape, F32)
            D[...] = jnp.zeros(D.shape, F32)
            VS[3] = jnp.zeros(VS.shape[1:], F32)
        for copy in flag_copies:
            copy.wait()
        if step == 0:
            ends_x = {-1: (X - 2, 0, 2), 0: (0, 2, X), 1: (0, X + 2, 2)}
            ends_y = {-1: (Y - 2, 0, 2), 0: (0, 2, Y), 1: (0, Y + 2, 2)}
            for d in range(8):
                from_x, to_x, n_x = ends_x[-SHIFT_X[d]]
                from_y, to_y, n_y = ends_y[-SHIFT_Y[d]]
                for x in range(n_x):
                    FL[to_x + x, to_y : to_y + n_y] = RF[d, from_x + x, from_y : from_y + n_y]
        for copy in copies:
            copy.wait()
        for n in range(4):
            for x in xs:
                low = RYL[n, x - lo]
                high = RYH[n, x - lo]
                if x < lo + w:
                    low = low + RC[0, n, x - lo]
                    high = high + RC[2, n, x - lo]
                if x >= X + lo:
                    low = low + RC[1, n, x - X - lo]
                    high = high + RC[3, n, x - X - lo]
                N[n, x, lo : lo + w] = N[n, x, lo : lo + w] + low
                N[n, x, Y + lo : Y + lo + w] = N[n, x, Y + lo : Y + lo + w] + high
        pack = jnp.zeros((YE, Z), F32)
        for x in xs:
            tot = []
            for n in range(4):
                v = N[n, x]
                if x < lo + 2 * h:
                    v = v + RXL[n, x - lo]
                if x >= X + lo:
                    v = v + RXH[n, x - X - lo]
                tot.append(v)
            fl = FL[x]
            inv = 1.0 / jnp.maximum(tot[0], MASS_FLOOR)
            for k in range(3):
                v = jnp.where(fl == 1.0, 0.0, tot[1 + k] * inv)
                if k == 2:
                    v = jnp.where(fl == 2.0, -PLATEN_SPEED, v)
                VZ[1, k, x] = v
                edge = jnp.where(is_low, pltpu.roll(v, 1, 1), v)
                l = k * XE + x
                moved = edge if l == 0 else pltpu.roll(edge, l, 1)
                pack = jnp.where(lane == l, moved, pack)
        PK[2 * step + 1] = pack
        copy = send(PK.at[2 * step + 1], PKR.at[2 * step + 1], base + 9, sibling)
        copy.wait()
        got = PKR[2 * step + 1]
        got = jnp.where(is_low, pltpu.roll(got, Z - 1, 1), got)
        got_high = jnp.where(is_low, got, 0.0)
        got_low = jnp.where(is_low, 0.0, got)
        for k in range(3):
            for x in xs:
                l = k * XE + x
                v = VZ[1, k, x]
                VZ[0, k, x] = jnp.where(lane == 0, unpack(got_low, l), pltpu.roll(v, 1, 1))
                VZ[2, k, x] = jnp.where(
                    lane == Z - 1, unpack(got_high, l), pltpu.roll(v, Z - 1, 1)
                )

        def body(x, carry):
            for c in range(3):
                for k in range(3):
                    for b in range(3):
                        VS[b, c, k, x] = VZ[c, k, x, 1 + b : 1 + b + Y]
                    if nb == 4:
                        VS[3, c, k, x, 0:1] = VZ[c, k, x, 0:1]
                        VS[3, c, k, x, Y - 1 : Y] = VZ[c, k, x, YE - 1 : YE]
            return carry

        lax.fori_loop(lo, X + 2 + h, body, 0)

    def gather(step):
        nab = 3 if step == 0 else 4

        def body(na, q, carry):
            i = q // S
            s = q % S
            side = i // (X - 1)
            wz = [PT[21 + c, q] for c in range(3)]
            wy = [PT[17 + b, q] for b in range(nab)]
            speed = [None] * 3
            mx = [None] * 3
            my = [None] * 3
            mz = [None] * 3

            def plus(total, term):
                return term if total is None else total + term

            for a in range(na):
                xi = i + 1 + a if a < 3 else side * (X + 3)
                u = [None] * 3
                uy = [None] * 3
                uz = [None] * 3
                for b in range(nab):
                    for k in range(3):
                        low = wz[0] * VS[b, 0, k, xi]
                        mid = wz[1] * VS[b, 1, k, xi]
                        high = wz[2] * VS[b, 2, k, xi]
                        t = wy[b] * (low + mid + high)
                        u[k] = plus(u[k], t)
                        if b == 0:
                            uy[k] = t
                        elif b == 2:
                            uy[k] = t - uy[k]
                        elif b == 3:
                            uy[k] = uy[k] + far_y * t
                        uz[k] = plus(uz[k], wy[b] * (high - low))
                wx = PT[13 + a, q]
                for k in range(3):
                    t = wx * u[k]
                    speed[k] = plus(speed[k], t)
                    if a == 0:
                        mx[k] = t
                    elif a == 2:
                        mx[k] = t - mx[k]
                    elif a == 3:
                        mx[k] = mx[k] + (4 * side - 2).astype(F32) * t
                    my[k] = plus(my[k], wx * uy[k])
                    mz[k] = plus(mz[k], wx * uz[k])
            moments = [mx, my, mz]
            if step == 0:
                state = [part[c, s, pl.ds(i, Y, stride=X), :] for c in range(22)]
            else:
                state = [ST[c, q] for c in range(22)]
            grad, div, stress = advance(state, speed, moments)
            if step == 0:
                for k in range(3):
                    ST[k, q] = state[k] + TIME_STEP * speed[k]
                    ST[3 + k, q] = speed[k]
                    for b in range(3):
                        ST[6 + 3 * k + b, q] = grad[k][b]
                for n in range(6):
                    ST[15 + n, q] = stress[n]
                ST[21, q] = state[21] * (1.0 + TIME_STEP * div)
            else:
                o = occ[s, pl.ds(i, Y, stride=X), :].astype(F32)
                stay = jnp.where(DM[q, 0:Y] < 0.5, o, 0.0)
                for n, v in enumerate(speed + stress):
                    out[n, s, pl.ds(i, Y, stride=X), :] = v * stay
                    VALS[n, q, 0:Y] = v * o
            return carry

        if step == 0:
            lax.fori_loop(0, R, functools.partial(body, 3), 0)
        else:
            edge_body = lambda t, carry: body(4, t + (t // S) * (R - 2 * S), carry)
            lax.fori_loop(0, 2 * S, edge_body, 0)
            lax.fori_loop(S, R - S, functools.partial(body, 3), 0)

    def extract():
        ks = lax.broadcasted_iota(jnp.int32, (Z, Z), 0).astype(F32)
        copies = []
        for first, count, ds in ((0, S, (0, 1, 2)), (R - S, S, (5, 6, 7)), (0, R, (3, 4))):
            rows = lax.broadcasted_iota(jnp.int32, (count * 8, Z), 0).astype(F32) + first * 8.0
            hot = jnp.concatenate(
                [jnp.where(ks == kidx[d : d + 1, :], 1.0, 0.0) for d in ds], axis=1
            ).astype(jnp.bfloat16)
            hot = jnp.concatenate([hot, hot], axis=0)
            for n in range(9):
                v = VALS[n, first : first + count].reshape(count * 8, Z)
                hi = v.astype(jnp.bfloat16)
                low = (v - hi.astype(F32)).astype(jnp.bfloat16)
                t = jnp.dot(
                    jnp.concatenate([hi, low], axis=1), hot, preferred_element_type=F32
                )
                for e, d in enumerate(ds):
                    here = rows == rowq[d : d + 1, :]
                    RES[d, n : n + 1] = jnp.sum(
                        jnp.where(here, t[:, e * Z : (e + 1) * Z], 0.0), axis=0, keepdims=True
                    )
            for d in ds:
                copies.append(
                    send(RES.at[d], ARR.at[d], 20 + d, at(SHIFT_X[d], SHIFT_Y[d]))
                )
        for copy in copies:
            copy.wait()
        for d in range(8):
            arr[:, d] = ARR[d]

    D[...] = jnp.zeros(D.shape, F32)
    prepare(0)
    deposit(3, 3 * X)
    combine(0, 3, N0)
    velocities(0, N0, SYH0, SYL0, RYL0, RYH0, RXL0, RXH0, RC0)
    gather(0)
    prepare(1)
    deposit(4, 3 * X + 2)
    combine(1, 4, N1)
    velocities(1, N1, SYH1, SYL1, RYL1, RYH1, RXL1, RXH1, RC1)
    gather(1)
    extract()


def body(n_gx, n_gy, particles, masses, occupied, node_flags, depart, arrive):
    _, S, X, Y, Z = particles.shape
    R, XE, YE = S * X, X + 4, Y + 4
    vmem = lambda *shape: pltpu.VMEM(shape, F32)
    final_state, arrivals = pl.pallas_call(
        functools.partial(kernel, S, X, Y, n_gx, n_gy),
        out_shape=(
            jax.ShapeDtypeStruct((9, S, Y * X, Z), F32),
            jax.ShapeDtypeStruct((9, 8, Z), F32),
        ),
        in_specs=[pl.BlockSpec(memory_space=pltpu.VMEM)] * 5,
        out_specs=(pl.BlockSpec(memory_space=pltpu.VMEM),) * 2,
        scratch_shapes=[
            vmem(22, R, Y, Z),
            vmem(24, R, Y, Z),
            vmem(4, 3, 4, XE, Y, Z),
            vmem(3, 4, XE, YE, Z),
            vmem(4, XE, YE, Z),
            vmem(4, XE, YE, Z),
            vmem(XE, YE, Z),
            vmem(3, 3, XE, YE, Z),
            vmem(4, 3, 3, XE, Y, Z),
            vmem(9, R, 8, Z),
            vmem(R, 8, Z),
            vmem(4, YE, Z),
            vmem(4, YE, Z),
            vmem(4, X + 2, 2, Z),
            vmem(4, X + 2, 2, Z),
            vmem(4, X + 2, 2, Z),
            vmem(4, X + 2, 2, Z),
            vmem(4, XE, 4, Z),
            vmem(4, XE, 4, Z),
            vmem(4, XE, 4, Z),
            vmem(4, XE, 4, Z),
            vmem(4, 2, YE, Z),
            vmem(4, 2, YE, Z),
            vmem(4, 4, YE, Z),
            vmem(4, 4, YE, Z),
            vmem(4, 4, 2, 2, Z),
            vmem(4, 4, 4, 4, Z),
            vmem(X, Y, Z),
            vmem(8, X, Y, Z),
            vmem(8, 9, Z),
            vmem(8, 9, Z),
            pltpu.SemaphoreType.DMA((36,)),
            pltpu.SemaphoreType.DMA((36,)),
        ],
        compiler_params=pltpu.CompilerParams(
            collective_id=0, has_side_effects=True, vmem_limit_bytes=60 * 1024 * 1024
        ),
        name="steps",
    )(
        particles.transpose(0, 1, 3, 2, 4).reshape(22, S, Y * X, Z),
        masses.transpose(0, 2, 1, 3).reshape(S, Y * X, Z),
        occupied.transpose(0, 2, 1, 3).reshape(S, Y * X, Z),
        node_flags.transpose(1, 0, 2).reshape(Y * X, Z),
        depart.reshape(8, Z),
    )
    final_state = final_state.reshape(9, S, Y, X, Z).transpose(0, 1, 3, 2, 4)
    return final_state, arrivals.reshape(9, 1, 1, 1, 8 * Z)


def solution(mesh):
    in_specs = (
        P(None, None, "gx", "gy", "col"),
        P(None, "gx", "gy", "col"),
        P(None, "gx", "gy", "col"),
        P("gx", "gy", "col"),
        P("gx", "gy", "col", None, None),
        P("gx", "gy", "col", None, None),
    )
    out_specs = (P(None, None, "gx", "gy", "col"), P(None, "gx", "gy", "col", None))
    sizes = mesh.shape
    assert sizes["col"] == 2
    return jax.shard_map(
        functools.partial(body, sizes["gx"], sizes["gy"]),
        mesh=mesh,
        in_specs=in_specs,
        out_specs=out_specs,
        check_vma=False,
    )
```
